128 devices in a mesh: band: 16 (over z_lo, x, core), col: 8 (over z_hi, y).
Axes of the slice: x: 4, y: 4, z: 4 (z_hi: 2, z_lo: 2; z = z_hi * 2 + z_lo), core: 2. Of those that a mesh axis runs over, the one named last changes fastest.
Arguments:
- bands: float32 [8192, 16384], P(('band', 'col')), may hold values from -6 to 6
- row_interp: float32 [16, 512, 640], P('band'), may hold values from -0.25 to 0.25
- col_interp: float32 [32, 640, 512], P('col'), may hold values from -0.25 to 0.25
- row_start: int32 [16], P('band'), may hold values from 0 to 128
- col_start: int32 [32], P('col'), may hold values from 0 to 128
- spacing: float32 [16], P('band'), may hold values from 0.5 to 2
Outputs:
- elevation: float32 [8192, 16384], P('band', 'col')
- slope_sine: float32 [8192, 16384], P('band', 'col')
- hillshade: float32 [8192, 16384], P('band', 'col')
The draws below stay inside these ranges and needn't reach their ends.
All inputs are finite; a program needn't handle non-finite values.
Results may differ from the reference program's by a relative error of at most 0.0003.
Values sent between devices are 32-bit elements; how exact they have to be, the bound alone decides.
A program may use at most 128 MiB of HBM per device.

```python
import math
import jax
import jax.numpy as jnp
from jax import lax

TILE = 512
MARGIN = 128
WIN = 640
TROWS = 16
TCOLS = 32
ROWS = 8192
COLS = 16384


def place_ends(entries, rng, least, high):
    extent = entries.shape
    spot = [jax.random.randint(jax.random.fold_in(rng, axis), (), 0, extent[axis]) for axis in range(len(extent))]
    entries = entries.at[tuple(spot)].set(least)
    longest = extent.index(max(extent))
    spot[longest] = (spot[longest] + 1) % extent[longest]
    return entries.at[tuple(spot)].set(high)


def level_of(own_key, extent, shards, least, largest):
    factor_of = 1.0
    for dim, shards_of in shards:
        draws = jax.random.uniform(jax.random.fold_in(jax.random.fold_in(own_key, 6), dim), (shards_of,), jnp.float32, least / len(shards), largest / len(shards))
        factor_of = factor_of * jnp.repeat(jnp.exp(draws), extent[dim] // shards_of).reshape((-1,) + (1,) * (len(extent) - 1 - dim))
    return factor_of


def centred(key, dims, scale, bound, cuts=(), held_as=jnp.bfloat16):
    result = scale * jax.random.normal(key, dims, jnp.float32)
    if cuts:
        result = result * level_of(key, dims, cuts, -0.22, 0.18)
    return jnp.clip(result, -bound, bound).astype(held_as)


def setup_inputs(seed: int = 0) -> dict:
    splits = jax.random.split(jax.random.key(seed), 7)
    return {
        "bands": centred(splits[0], (ROWS, COLS), 1.0, 6.0, ((0, 128),), jnp.float32),
        "row_interp": centred(splits[1], (TROWS, TILE, WIN), WIN ** -0.5, 0.25, ((0, 16),), jnp.float32),
        "col_interp": centred(splits[2], (TCOLS, WIN, TILE), WIN ** -0.5, 0.25, ((0, 8),), jnp.float32),
        "row_start": place_ends(jax.random.randint(splits[3], (TROWS,), 0, TILE + 2 * MARGIN - WIN + 1), jax.random.fold_in(splits[3], 1), 0, TILE + 2 * MARGIN - WIN).astype(jnp.int32),
        "col_start": place_ends(jax.random.randint(splits[4], (TCOLS,), 0, TILE + 2 * MARGIN - WIN + 1), jax.random.fold_in(splits[4], 1), 0, TILE + 2 * MARGIN - WIN).astype(jnp.int32),
        "spacing": jnp.clip(jnp.exp(math.log(2.0) - 1.3862944 * jax.random.uniform(splits[5], (TROWS,), jnp.float32) ** level_of(splits[5], (TROWS,), ((0, 16),), -0.2, 0.2)), 0.5, 2.0),
    }


def horn(elevation, spacing):
    z = jnp.pad(elevation, 1)
    scale = 8.0 * jnp.repeat(spacing, TILE)[:, None]
    right = z[:-2, 2:] + 2.0 * z[1:-1, 2:] + z[2:, 2:]
    left = z[:-2, :-2] + 2.0 * z[1:-1, :-2] + z[2:, :-2]
    lower = z[2:, :-2] + 2.0 * z[2:, 1:-1] + z[2:, 2:]
    upper = z[:-2, :-2] + 2.0 * z[:-2, 1:-1] + z[:-2, 2:]
    grad_p = (right - left) / scale
    grad_q = (lower - upper) / scale
    total = grad_p * grad_p + grad_q * grad_q
    denom = jnp.sqrt(1.0 + total)
    slope_sine = jnp.sqrt(total) / denom
    hillshade = (0.70710678 - 0.5 * grad_p + 0.5 * grad_q) / denom
    return (slope_sine, hillshade)

def reference(bands, row_interp, col_interp, row_start, col_start, spacing):
    padded = jnp.pad(bands, MARGIN)
    tcount = col_interp.shape[0]

    def one_row(index):
        start = (index * TILE + row_start[index]).astype(jnp.int32)
        window = lax.dynamic_slice_in_dim(padded, start, WIN, 0)
        rowres = jnp.dot(row_interp[index], window, precision=lax.Precision.HIGHEST, preferred_element_type=jnp.float32)

        def one_col(jindex):
            cstart = (jindex * TILE + col_start[jindex]).astype(jnp.int32)
            cols = lax.dynamic_slice_in_dim(rowres, cstart, WIN, 1)
            return jnp.dot(cols, col_interp[jindex], precision=lax.Precision.HIGHEST, preferred_element_type=jnp.float32)
        tiles = lax.map(one_col, jnp.arange(tcount, dtype=jnp.int32))
        return jnp.moveaxis(tiles, 0, 1).reshape(TILE, tcount * TILE)
    elevation = lax.map(one_row, jnp.arange(row_interp.shape[0], dtype=jnp.int32))
    elevation = elevation.reshape(row_interp.shape[0] * TILE, tcount * TILE)
    slope_sine, hillshade = horn(elevation, spacing)
    return (elevation, slope_sine, hillshade)
```

```python
import jax
import jax.numpy as jnp
from jax import lax
from jax.experimental import pallas as pl
from jax.experimental.pallas import tpu as pltpu
from jax.sharding import PartitionSpec as P

MESH = pl.DeviceIdType.MESH
F32, BF16 = jnp.float32, jnp.bfloat16

TILE, WIN, MARGIN = 512, 640, 128
NB, NC, NT = 16, 8, 4
COLS = 16384
BLOCK = TILE * NT
SPAN = TILE + 2 * MARGIN
EXT = BLOCK + 2 * MARGIN
SRC = TILE // NC
Z = TILE + 16

GROUPS = (
    ((0, 128, 384, 640, 768), 0),
    ((1536, 1664, 1920, 2176, 2304), 3),
    ((768, 1024, 1280), 1),
    ((1280, 1536), 2),
)
HORN = ((), (), ((0, 768), (768, 896), (1664, 2048)), ((896, 1664),))


def split(x):
    high = x.astype(BF16)
    return high, (x - high.astype(F32)).astype(BF16)


def dot(a, b):
    return lax.dot_general(a, b, (((1,), (0,)), ((), ())), preferred_element_type=F32)


def dot3(ah, al, bh, bl):
    return dot(ah, bh) + dot(ah, bl) + dot(al, bh)


def gather_kernel(
    row_start, col_start, spacing, bands, row_interp, col_interp,
    oz, osl, ohi,
    ext, z, rmat, cmat, rh, rl, ch, cl, wh, wl, left, right, lsend, rsend, vz, vs, vh,
    send_sem, recv_sem, own_sem, mat_sem, up_send, up_recv, dn_send, dn_recv,
    eu_send, eu_recv, ed_send, ed_recv, side_send, side_recv, corner_send, corner_recv, out_sem,
):
    b, c = lax.axis_index("band"), lax.axis_index("col")
    zh, y = c // 4, lax.rem(c, 4)

    def peer(s):
        return lax.rem(zh + lax.rem(s, 2), 2) * 4 + lax.rem(y + s // 2, 4)

    def at(db, dc):
        return {"band": b + db, "col": c + dc}

    def exists(db, dc):
        ok = jnp.bool_(True)
        if db < 0:
            ok = b > 0
        if db > 0:
            ok = b < NB - 1
        if dc < 0:
            ok = jnp.logical_and(ok, c > 0)
        if dc > 0:
            ok = jnp.logical_and(ok, c < NC - 1)
        return ok

    z[0:8, :] = jnp.zeros((8, EXT), F32)
    z[Z - 8 : Z, :] = jnp.zeros((8, EXT), F32)
    left[...] = jnp.zeros_like(left)
    right[...] = jnp.zeros_like(right)

    barrier = pltpu.get_barrier_semaphore()

    def greet(s, carry):
        pl.semaphore_signal(barrier, 1, device_id={"col": peer(s)}, device_id_type=MESH)
        return carry

    lax.fori_loop(1, NC, greet, 0)
    near = [(db, dc) for db in (-1, 1) for dc in (-1, 0, 1)]
    for db, dc in near:
        @pl.when(exists(db, dc))
        def _():
            pl.semaphore_signal(barrier, 1, device_id=at(db, dc), device_id_type=MESH)
    rows_near = (b > 0).astype(jnp.int32) + (b < NB - 1).astype(jnp.int32)
    cols_near = (c > 0).astype(jnp.int32) + (c < NC - 1).astype(jnp.int32)
    pl.semaphore_wait(barrier, NC - 1 + rows_near * (1 + cols_near))

    mine = pl.ds(pl.multiple_of(c * SRC, SRC), SRC)
    for g, (edges, _) in enumerate(GROUPS):
        for lo, hi in zip(edges[:-1], edges[1:]):
            def source(dst):
                start = lax.rem(dst * BLOCK + (lo + COLS - MARGIN), COLS)
                return bands.at[:, pl.ds(pl.multiple_of(start, 128), hi - lo)]

            def send(s, carry):
                dst = peer(s)
                pltpu.make_async_remote_copy(
                    source(dst), ext.at[mine, lo:hi], send_sem.at[g], recv_sem.at[g, c],
                    device_id={"col": dst}, device_id_type=MESH,
                ).start()
                return carry

            lax.fori_loop(1, NC, send, 0)
            pltpu.make_async_copy(source(c), ext.at[mine, lo:hi], own_sem.at[g]).start()

    rcopy = pltpu.make_async_copy(row_interp.at[0], rmat, mat_sem.at[0])
    ccopy = pltpu.make_async_copy(col_interp, cmat, mat_sem.at[1])
    rcopy.start()
    ccopy.start()

    @pl.when(b == 0)
    def _():
        ext[TILE : TILE + MARGIN, :] = jnp.zeros((MARGIN, EXT), F32)

    @pl.when(b == NB - 1)
    def _():
        ext[TILE + MARGIN :, :] = jnp.zeros((MARGIN, EXT), F32)

    rcopy.wait()
    ah, al = split(rmat[...])
    r0 = row_start[0]
    for k in range(3):
        m = lax.broadcasted_iota(jnp.int32, (WIN, 256), 1) + k * 256
        row = m + MARGIN if k < 2 else jnp.where(m < TILE + MARGIN, m - TILE, m)
        hot = jnp.where(row - r0 == lax.broadcasted_iota(jnp.int32, (WIN, 256), 0), 1.0, 0.0).astype(BF16)
        rh[:, k * 256 : (k + 1) * 256] = dot(ah, hot).astype(BF16)
        rl[:, k * 256 : (k + 1) * 256] = dot(al, hot).astype(BF16)

    ccopy.wait()
    for j in range(NT):
        c0 = col_start[j]
        low = jnp.where(c == 0, MARGIN, 0) if j == 0 else 0
        high = jnp.where(c == NC - 1, TILE + MARGIN, SPAN) if j == NT - 1 else SPAN

        def move(k, carry):
            base = pl.multiple_of(k * 256, 256)
            ah, al = split(cmat[j])
            m = lax.broadcasted_iota(jnp.int32, (256, WIN), 0) + base
            hit = m - c0 == lax.broadcasted_iota(jnp.int32, (256, WIN), 1)
            hit = jnp.logical_and(hit, jnp.logical_and(m >= low, m < high))
            hot = jnp.where(hit, 1.0, 0.0).astype(BF16)
            ch[j, pl.ds(base, 256), :] = dot(hot, ah).astype(BF16)
            cl[j, pl.ds(base, 256), :] = dot(hot, al).astype(BF16)
            return carry

        lax.fori_loop(0, SPAN // 256, move, 0)

    inv = jnp.tile(1.0 / jnp.full((16, 128), 8.0 * spacing[0], F32), (1, 3))
    outs = []

    def edge(ref_from, ref_to, sends, recvs, db, dc):
        return pltpu.make_async_remote_copy(
            ref_from, ref_to, sends, recvs, device_id=at(db, dc), device_id_type=MESH
        )

    waits = []
    for g, (edges, tile) in enumerate(GROUPS):
        lo, hi = edges[0], edges[-1]
        cols = slice(lo, hi)

        def arrive(s, carry):
            src = peer(s)
            rows = ext.at[pl.ds(pl.multiple_of(src * SRC, SRC), SRC), cols]
            pltpu.make_async_remote_copy(
                rows, rows, send_sem.at[g], recv_sem.at[g, src], device_id={"col": src}, device_id_type=MESH
            ).wait_recv()
            return carry

        lax.fori_loop(1, NC, arrive, 0)
        pltpu.make_async_copy(ext.at[mine, cols], ext.at[mine, cols], own_sem.at[g]).wait()

        down = edge(ext.at[TILE - MARGIN : TILE, cols], ext.at[TILE : TILE + MARGIN, cols], dn_send.at[g], dn_recv.at[g], 1, 0)
        upward = edge(ext.at[0:MARGIN, cols], ext.at[TILE + MARGIN : SPAN, cols], up_send.at[g], up_recv.at[g], -1, 0)
        pl.when(b < NB - 1)(down.start)
        pl.when(b > 0)(upward.start)
        pl.when(b > 0)(down.wait_recv)
        pl.when(b < NB - 1)(upward.wait_recv)

        def rows_of(n, carry):
            at_n = pl.ds(pl.multiple_of(lo + n * 256, 256), 256)
            xh, xl = split(ext[:, at_n])
            part = dot3(rh[...], rl[...], xh, xl)
            high, low = split(part)
            wh[:, at_n] = high
            wl[:, at_n] = low
            return carry

        lax.fori_loop(0, (hi - lo) // 256, rows_of, 0)

        def cols_of(n, carry):
            at_n = pl.ds(pl.multiple_of(n * 256, 256), 256)
            part = dot3(wh[:, tile * TILE : tile * TILE + SPAN], wl[:, tile * TILE : tile * TILE + SPAN], ch[tile, :, at_n], cl[tile, :, at_n])
            z[8 : 8 + TILE, pl.ds(pl.multiple_of(MARGIN + tile * TILE + n * 256, 128), 256)] = part
            return carry

        lax.fori_loop(0, TILE // 256, cols_of, 0)

        tc = slice(MARGIN + tile * TILE, MARGIN + (tile + 1) * TILE)
        first, last = slice(8, 16), slice(TILE, TILE + 8)
        top, bottom = slice(0, 8), slice(Z - 8, Z)
        pairs = [
            (edge(z.at[last, tc], z.at[top, tc], ed_send.at[tile], ed_recv.at[tile], 1, 0), (1, 0)),
            (edge(z.at[first, tc], z.at[bottom, tc], eu_send.at[tile], eu_recv.at[tile], -1, 0), (-1, 0)),
        ]
        if tile == 0:
            near_cols, far_cols, dc = slice(MARGIN, 2 * MARGIN), slice(EXT - MARGIN, EXT), -1
            lsend[...] = jnp.transpose(z[8 : 8 + TILE, near_cols])[0:8, :]
            pairs.append((edge(lsend, right.at[0:8, :], side_send.at[0], side_recv.at[0], 0, -1), (0, -1)))
        if tile == NT - 1:
            near_cols, far_cols, dc = slice(BLOCK, BLOCK + MARGIN), slice(0, MARGIN), 1
            rsend[...] = jnp.transpose(z[8 : 8 + TILE, near_cols])[120:128, :]
            pairs.append((edge(rsend, left.at[120:128, :], side_send.at[1], side_recv.at[1], 0, 1), (0, 1)))
        if tile in (0, NT - 1):
            i = 0 if tile == 0 else 2
            pairs.append((edge(z.at[last, near_cols], z.at[top, far_cols], corner_send.at[i], corner_recv.at[i], 1, dc), (1, dc)))
            pairs.append((edge(z.at[first, near_cols], z.at[bottom, far_cols], corner_send.at[i + 1], corner_recv.at[i + 1], -1, dc), (-1, dc)))
        for copy, way in pairs:
            pl.when(exists(*way))(copy.start)
        waits.extend(pairs)

        if not HORN[g]:
            continue
        for copy, way in waits:
            pl.when(exists(-way[0], -way[1]))(copy.wait_recv)
            pl.when(exists(*way))(copy.wait_send)
        waits = []
        if g == 2:
            z[8 : 8 + TILE, 0:MARGIN] = jnp.transpose(left[...])
            z[8 : 8 + TILE, EXT - MARGIN : EXT] = jnp.transpose(right[...])
        for first_col, last_col in HORN[g]:
            width = 384 if (last_col - first_col) % 384 == 0 else 128
            span = width + 256

            def strip(i, carry):
                r = pl.multiple_of(i * 16, 16)

                def chunk(n, carry):
                    at_n = pl.multiple_of(first_col + n * width, 128)
                    blk = z[pl.ds(r, 32), pl.ds(at_n, span)]
                    up, mid, dn = blk[7:23], blk[8:24], blk[9:25]
                    s = up + dn + 2.0 * mid
                    d = dn - up
                    sc = inv[:, :width]
                    p = (pltpu.roll(s, span - 1, 1) - pltpu.roll(s, 1, 1))[:, 128 : 128 + width] * sc
                    q = (pltpu.roll(d, span - 1, 1) + pltpu.roll(d, 1, 1) + 2.0 * d)[:, 128 : 128 + width] * sc
                    t = p * p + q * q
                    f = lax.rsqrt(1.0 + t)
                    o = (pl.ds(r, 16), pl.ds(at_n, width))
                    vz[o] = mid[:, 128 : 128 + width]
                    vs[o] = jnp.sqrt(t) * f
                    vh[o] = (0.70710678 + 0.5 * (q - p)) * f
                    return carry

                return lax.fori_loop(0, (last_col - first_col) // width, chunk, carry)

            lax.fori_loop(0, TILE // 16, strip, 0)
            cs = slice(first_col, last_col)
            for k, (v, o) in enumerate(((vz, oz), (vs, osl), (vh, ohi))):
                copy = pltpu.make_async_copy(v.at[:, cs], o.at[:, cs], out_sem.at[len(outs)])
                copy.start()
                outs.append(copy)

    for g, (edges, _) in enumerate(GROUPS):
        lo, hi = edges[0], edges[-1]
        cols = slice(lo, hi)
        gone = ext.at[0 : (NC - 1) * SRC, cols]
        pltpu.make_async_remote_copy(
            gone, gone, send_sem.at[g], recv_sem.at[g, c], device_id={"col": peer(1)}, device_id_type=MESH
        ).wait_send()
        down = edge(ext.at[TILE - MARGIN : TILE, cols], ext.at[TILE : TILE + MARGIN, cols], dn_send.at[g], dn_recv.at[g], 1, 0)
        upward = edge(ext.at[0:MARGIN, cols], ext.at[TILE + MARGIN : SPAN, cols], up_send.at[g], up_recv.at[g], -1, 0)
        pl.when(b < NB - 1)(down.wait_send)
        pl.when(b > 0)(upward.wait_send)
    for copy in outs:
        copy.wait()


def on_device(bands, row_interp, col_interp, row_start, col_start, spacing):
    out = jax.ShapeDtypeStruct((TILE, BLOCK), F32)
    smem, anywhere = pl.BlockSpec(memory_space=pltpu.SMEM), pl.BlockSpec(memory_space=pl.ANY)
    vmem, dma = pltpu.VMEM, pltpu.SemaphoreType.DMA
    ng = len(GROUPS)
    return pl.pallas_call(
        gather_kernel,
        out_shape=(out,) * 3,
        in_specs=[smem] * 3 + [anywhere] * 3,
        out_specs=(anywhere,) * 3,
        scratch_shapes=[
            vmem((SPAN, EXT), F32), vmem((Z, EXT), F32),
            vmem((TILE, WIN), F32), vmem((NT, WIN, TILE), F32),
            vmem((TILE, SPAN), BF16), vmem((TILE, SPAN), BF16),
            vmem((NT, SPAN, TILE), BF16), vmem((NT, SPAN, TILE), BF16),
            vmem((TILE, EXT), BF16), vmem((TILE, EXT), BF16),
            vmem((MARGIN, TILE), F32), vmem((MARGIN, TILE), F32),
            vmem((8, TILE), F32), vmem((8, TILE), F32),
            vmem((TILE, BLOCK), F32), vmem((TILE, BLOCK), F32), vmem((TILE, BLOCK), F32),
            dma((ng,)), dma((ng, NC)), dma((ng,)), dma((2,)),
            dma((ng,)), dma((ng,)), dma((ng,)), dma((ng,)),
            dma((NT,)), dma((NT,)), dma((NT,)), dma((NT,)),
            dma((2,)), dma((2,)), dma((4,)), dma((4,)), dma((12,)),
        ],
        compiler_params=pltpu.CompilerParams(
            collective_id=0, has_side_effects=True, vmem_limit_bytes=60 * 2**20
        ),
    )(row_start, col_start, spacing, bands, row_interp, col_interp)


def solution(mesh):
    in_specs = (
        P(("band", "col"), None),
        P("band", None, None),
        P("col", None, None),
        P("band"),
        P("col"),
        P("band"),
    )
    out_specs = (P("band", "col"), P("band", "col"), P("band", "col"))
    return jax.shard_map(
        on_device, mesh=mesh, in_specs=in_specs, out_specs=out_specs, check_vma=False
    )
```

```python
import jax
import jax.numpy as jnp
from jax import lax
from jax.experimental import pallas as pl
from jax.experimental.pallas import tpu as pltpu
from jax.sharding import PartitionSpec as P

MESH = pl.DeviceIdType.MESH
F32, BF16 = jnp.float32, jnp.bfloat16

TILE, WIN, MARGIN = 512, 640, 128
NB, NC, NT = 16, 8, 4
COLS = 16384
BLOCK = TILE * NT
SPAN = TILE + 2 * MARGIN
EXT = BLOCK + 2 * MARGIN
SRC = TILE // NC
Z = TILE + 16

UNITS = (
    (0, 128, 256),
    (256, 512, 768),
    (1536, 1792),
    (1792, 2048, 2176, 2304),
    (768, 1024),
    (1024, 1280),
    (1280, 1536),
)
AHEAD = 3
DONE = {1: 0, 3: 3, 5: 1, 6: 2}
HORN = {3: (0, ((128, 384),)), 1: (3, ((0, 128), (1664, 2048))), 2: (1, ((384, 896),))}
LATE = (896, 1664)
KERNEL_VMEM = 47 * 2**20
TINY = 1.1754944e-38


def split(x):
    high = x.astype(BF16)
    return high, (x - high.astype(F32)).astype(BF16)


def dot(a, b):
    return lax.dot_general(a, b, (((1,), (0,)), ((), ())), preferred_element_type=F32)


def dot3(ah, al, bh, bl):
    return dot(ah, bh) + dot(ah, bl) + dot(al, bh)


def horn(z, inv, r, lo, width):
    span = width + 2 * MARGIN
    blk = z[pl.ds(r, 32), lo : lo + span]
    up, mid, dn = blk[7:23], blk[8:24], blk[9:25]
    s = up + dn + 2.0 * mid
    d = dn - up
    sc = jnp.tile(inv, (1, width // 128))
    keep = slice(MARGIN, MARGIN + width)
    p = (pltpu.roll(s, span - 1, 1) - pltpu.roll(s, 1, 1))[:, keep] * sc
    q = (pltpu.roll(d, span - 1, 1) + pltpu.roll(d, 1, 1) + 2.0 * d)[:, keep] * sc
    t = p * p + q * q
    u = 1.0 + t
    f = lax.rsqrt(u)
    return t * lax.rsqrt(jnp.maximum(t * u, TINY)), (0.70710678 + 0.5 * (q - p)) * f


def inverse(spacing):
    return 1.0 / jnp.full((16, 128), 8.0 * spacing[0], F32)


def gather_kernel(
    row_start, col_start, spacing, bands, row_interp, col_interp,
    z, vs, vh,
    ext, rmat, cmat, rh, rl, ch, cl, wh, wl, left, right, lsend, rsend,
    send_sem, recv_sem, own_sem, mat_sem, up_send, up_recv, dn_send, dn_recv,
    eu_send, eu_recv, ed_send, ed_recv, side_send, side_recv, corner_send, corner_recv,
):
    b, c = lax.axis_index("band"), lax.axis_index("col")
    zh, y = c // 4, lax.rem(c, 4)

    def peer(s):
        return lax.rem(zh + lax.rem(s, 2), 2) * 4 + lax.rem(y + s // 2, 4)

    def at(db, dc):
        return {"band": b + db, "col": c + dc}

    def exists(db, dc):
        ok = jnp.bool_(True)
        if db < 0:
            ok = b > 0
        if db > 0:
            ok = b < NB - 1
        if dc < 0:
            ok = jnp.logical_and(ok, c > 0)
        if dc > 0:
            ok = jnp.logical_and(ok, c < NC - 1)
        return ok

    z[0:8, :] = jnp.zeros((8, EXT), F32)
    z[Z - 8 : Z, :] = jnp.zeros((8, EXT), F32)
    left[...] = jnp.zeros_like(left)
    right[...] = jnp.zeros_like(right)

    barrier = pltpu.get_barrier_semaphore()

    def greet(s, carry):
        pl.semaphore_signal(barrier, 1, device_id={"col": peer(s)}, device_id_type=MESH)
        return carry

    lax.fori_loop(1, NC, greet, 0)
    near = [(db, dc) for db in (-1, 1) for dc in (-1, 0, 1)]
    for db, dc in near:
        @pl.when(exists(db, dc))
        def _():
            pl.semaphore_signal(barrier, 1, device_id=at(db, dc), device_id_type=MESH)
    rows_near = (b > 0).astype(jnp.int32) + (b < NB - 1).astype(jnp.int32)
    cols_near = (c > 0).astype(jnp.int32) + (c < NC - 1).astype(jnp.int32)
    pl.semaphore_wait(barrier, NC - 1 + rows_near * (1 + cols_near))

    mine = pl.ds(pl.multiple_of(c * SRC, SRC), SRC)
    def post(g):
        edges = UNITS[g]
        for lo, hi in zip(edges[:-1], edges[1:]):
            def source(dst, lo=lo, hi=hi):
                start = lax.rem(dst * BLOCK + (lo + COLS - MARGIN), COLS)
                return bands.at[:, pl.ds(pl.multiple_of(start, 128), hi - lo)]

            def send(s, carry, lo=lo, hi=hi, source=source):
                dst = peer(s)
                pltpu.make_async_remote_copy(
                    source(dst), ext.at[mine, lo:hi], send_sem.at[g], recv_sem.at[g, c],
                    device_id={"col": dst}, device_id_type=MESH,
                ).start()
                return carry

            lax.fori_loop(1, NC, send, 0)
            pltpu.make_async_copy(source(c), ext.at[mine, lo:hi], own_sem.at[g]).start()

    for g in range(AHEAD):
        post(g)

    rcopy = pltpu.make_async_copy(row_interp.at[0], rmat, mat_sem.at[0])
    ccopy = pltpu.make_async_copy(col_interp, cmat, mat_sem.at[1])
    rcopy.start()
    ccopy.start()

    @pl.when(b == 0)
    def _():
        ext[TILE : TILE + MARGIN, :] = jnp.zeros((MARGIN, EXT), F32)

    @pl.when(b == NB - 1)
    def _():
        ext[TILE + MARGIN :, :] = jnp.zeros((MARGIN, EXT), F32)

    rcopy.wait()
    ah, al = split(rmat[...])
    r0 = row_start[0]
    for k in range(3):
        m = lax.broadcasted_iota(jnp.int32, (WIN, 256), 1) + k * 256
        row = m + MARGIN if k < 2 else jnp.where(m < TILE + MARGIN, m - TILE, m)
        hot = jnp.where(row - r0 == lax.broadcasted_iota(jnp.int32, (WIN, 256), 0), 1.0, 0.0).astype(BF16)
        rh[:, k * 256 : (k + 1) * 256] = dot(ah, hot).astype(BF16)
        rl[:, k * 256 : (k + 1) * 256] = dot(al, hot).astype(BF16)

    ccopy.wait()
    for j in range(NT):
        c0 = col_start[j]
        low = jnp.where(c == 0, MARGIN, 0) if j == 0 else 0
        high = jnp.where(c == NC - 1, TILE + MARGIN, SPAN) if j == NT - 1 else SPAN

        def move(k, carry):
            base = pl.multiple_of(k * 256, 256)
            ah, al = split(cmat[j])
            m = lax.broadcasted_iota(jnp.int32, (256, WIN), 0) + base
            hit = m - c0 == lax.broadcasted_iota(jnp.int32, (256, WIN), 1)
            hit = jnp.logical_and(hit, jnp.logical_and(m >= low, m < high))
            hot = jnp.where(hit, 1.0, 0.0).astype(BF16)
            ch[j, pl.ds(base, 256), :] = dot(hot, ah).astype(BF16)
            cl[j, pl.ds(base, 256), :] = dot(hot, al).astype(BF16)
            return carry

        lax.fori_loop(0, SPAN // 256, move, 0)

    inv = inverse(spacing)

    def edge(ref_from, ref_to, sends, recvs, db, dc):
        return pltpu.make_async_remote_copy(
            ref_from, ref_to, sends, recvs, device_id=at(db, dc), device_id_type=MESH
        )

    def relays(g):
        cols = slice(UNITS[g][0], UNITS[g][-1])
        down = edge(ext.at[TILE - MARGIN : TILE, cols], ext.at[TILE : TILE + MARGIN, cols], dn_send.at[g], dn_recv.at[g], 1, 0)
        upward = edge(ext.at[0:MARGIN, cols], ext.at[TILE + MARGIN : SPAN, cols], up_send.at[g], up_recv.at[g], -1, 0)
        return down, upward

    def arrive(g):
        cols = slice(UNITS[g][0], UNITS[g][-1])

        def one(s, carry):
            src = peer(s)
            rows = ext.at[pl.ds(pl.multiple_of(src * SRC, SRC), SRC), cols]
            pltpu.make_async_remote_copy(
                rows, rows, send_sem.at[g], recv_sem.at[g, src], device_id={"col": src}, device_id_type=MESH
            ).wait_recv()
            return carry

        lax.fori_loop(1, NC, one, 0)
        pltpu.make_async_copy(ext.at[mine, cols], ext.at[mine, cols], own_sem.at[g]).wait()
        down, upward = relays(g)
        pl.when(b < NB - 1)(down.start)
        pl.when(b > 0)(upward.start)
        if g + AHEAD < len(UNITS):
            post(g + AHEAD)

    def finish(pairs):
        for copy, way in pairs:
            pl.when(exists(-way[0], -way[1]))(copy.wait_recv)
            pl.when(exists(*way))(copy.wait_send)

    waits = {}
    arrive(0)
    for g in range(len(UNITS)):
        lo, hi = UNITS[g][0], UNITS[g][-1]
        tile = DONE.get(g)
        if g + 1 < len(UNITS):
            arrive(g + 1)
        down, upward = relays(g)
        pl.when(b > 0)(down.wait_recv)
        pl.when(b < NB - 1)(upward.wait_recv)

        def rows_of(n, carry):
            at_n = pl.ds(pl.multiple_of(lo + n * 256, 256), 256)
            xh, xl = split(ext[:, at_n])
            part = dot3(rh[...], rl[...], xh, xl)
            high, low = split(part)
            wh[:, at_n] = high
            wl[:, at_n] = low
            return carry

        lax.fori_loop(0, (hi - lo) // 256, rows_of, 0)
        if tile is None:
            continue

        def cols_of(n, carry):
            at_n = pl.ds(pl.multiple_of(n * 256, 256), 256)
            part = dot3(wh[:, tile * TILE : tile * TILE + SPAN], wl[:, tile * TILE : tile * TILE + SPAN], ch[tile, :, at_n], cl[tile, :, at_n])
            z[8 : 8 + TILE, pl.ds(pl.multiple_of(MARGIN + tile * TILE + n * 256, 128), 256)] = part
            return carry

        lax.fori_loop(0, TILE // 256, cols_of, 0)

        tc = slice(MARGIN + tile * TILE, MARGIN + (tile + 1) * TILE)
        first, last = slice(8, 16), slice(TILE, TILE + 8)
        top, bottom = slice(0, 8), slice(Z - 8, Z)
        pairs = [
            (edge(z.at[last, tc], z.at[top, tc], ed_send.at[tile], ed_recv.at[tile], 1, 0), (1, 0)),
            (edge(z.at[first, tc], z.at[bottom, tc], eu_send.at[tile], eu_recv.at[tile], -1, 0), (-1, 0)),
        ]
        if tile == 0:
            near_cols, far_cols, dc = slice(MARGIN, 2 * MARGIN), slice(EXT - MARGIN, EXT), -1
            lsend[...] = jnp.transpose(z[8 : 8 + TILE, near_cols])[0:8, :]
            pairs.append((edge(lsend, right.at[0:8, :], side_send.at[0], side_recv.at[0], 0, -1), (0, -1)))
        if tile == NT - 1:
            near_cols, far_cols, dc = slice(BLOCK, BLOCK + MARGIN), slice(0, MARGIN), 1
            rsend[...] = jnp.transpose(z[8 : 8 + TILE, near_cols])[120:128, :]
            pairs.append((edge(rsend, left.at[120:128, :], side_send.at[1], side_recv.at[1], 0, 1), (0, 1)))
        if tile in (0, NT - 1):
            i = 0 if tile == 0 else 2
            pairs.append((edge(z.at[last, near_cols], z.at[top, far_cols], corner_send.at[i], corner_recv.at[i], 1, dc), (1, dc)))
            pairs.append((edge(z.at[first, near_cols], z.at[bottom, far_cols], corner_send.at[i + 1], corner_recv.at[i + 1], -1, dc), (-1, dc)))
        for copy, way in pairs:
            pl.when(exists(*way))(copy.start)
        waits[tile] = pairs

        if tile not in HORN:
            continue
        ready, spans = HORN[tile]
        finish(waits.pop(ready))
        if ready == 3:
            z[8 : 8 + TILE, 0:MARGIN] = jnp.transpose(left[...])
            z[8 : 8 + TILE, EXT - MARGIN : EXT] = jnp.transpose(right[...])

        def strip(i, carry):
            r = pl.multiple_of(i * 16, 16)
            for first_col, last_col in spans:
                o = (pl.ds(r, 16), slice(first_col, last_col))
                vs[o], vh[o] = horn(z, inv, r, first_col, last_col - first_col)
            return carry

        lax.fori_loop(0, TILE // 16, strip, 0)

    for pairs in waits.values():
        finish(pairs)
    for g in range(len(UNITS)):
        cols = slice(UNITS[g][0], UNITS[g][-1])
        gone = ext.at[0 : (NC - 1) * SRC, cols]
        pltpu.make_async_remote_copy(
            gone, gone, send_sem.at[g], recv_sem.at[g, c], device_id={"col": peer(1)}, device_id_type=MESH
        ).wait_send()
        down, upward = relays(g)
        pl.when(b < NB - 1)(down.wait_send)
        pl.when(b > 0)(upward.wait_send)


def write_kernel(spacing, z, vs, vh, oz, osl, ohi, hs, hh, sem, late_sem):
    copies = [pltpu.make_async_copy(z.at[8 : 8 + TILE, MARGIN : MARGIN + BLOCK], oz, sem.at[4])]
    for k, (v, o) in enumerate(((vs, osl), (vh, ohi))):
        for n, cs in enumerate((slice(0, LATE[0]), slice(LATE[1], BLOCK))):
            copies.append(pltpu.make_async_copy(v.at[:, cs], o.at[:, cs], sem.at[2 * k + n]))
    for copy in copies:
        copy.start()
    inv = inverse(spacing)
    parts = 4
    for part in range(parts):
        def strip(i, carry):
            r = pl.multiple_of(i * 16, 16)
            for lo in range(LATE[0], LATE[1], 384):
                o = (pl.ds(r, 16), slice(lo - LATE[0], lo - LATE[0] + 384))
                hs[o], hh[o] = horn(z, inv, r, lo, 384)
            return carry

        first, last = part * TILE // parts, (part + 1) * TILE // parts
        lax.fori_loop(first // 16, last // 16, strip, 0)
        for k, (v, o) in enumerate(((hs, osl), (hh, ohi))):
            copy = pltpu.make_async_copy(v.at[first:last], o.at[first:last, LATE[0] : LATE[1]], late_sem.at[k, part])
            copy.start()
            copies.append(copy)
    for copy in copies:
        copy.wait()


def on_device(bands, row_interp, col_interp, row_start, col_start, spacing):
    out = jax.ShapeDtypeStruct((TILE, BLOCK), F32)
    smem, anywhere = pl.BlockSpec(memory_space=pltpu.SMEM), pl.BlockSpec(memory_space=pl.ANY)
    vmem, dma = pltpu.VMEM, pltpu.SemaphoreType.DMA
    nu = len(UNITS)
    in_vmem = pl.BlockSpec(memory_space=pltpu.VMEM)
    z, vs, vh = pl.pallas_call(
        gather_kernel,
        out_shape=(vmem((Z, EXT), F32), vmem((TILE, BLOCK), F32), vmem((TILE, BLOCK), F32)),
        in_specs=[smem] * 3 + [anywhere] * 3,
        out_specs=(in_vmem,) * 3,
        scratch_shapes=[
            vmem((SPAN, EXT), F32),
            vmem((TILE, WIN), F32), vmem((NT, WIN, TILE), F32),
            vmem((TILE, SPAN), BF16), vmem((TILE, SPAN), BF16),
            vmem((NT, SPAN, TILE), BF16), vmem((NT, SPAN, TILE), BF16),
            vmem((TILE, EXT), BF16), vmem((TILE, EXT), BF16),
            vmem((MARGIN, TILE), F32), vmem((MARGIN, TILE), F32),
            vmem((8, TILE), F32), vmem((8, TILE), F32),
            dma((nu,)), dma((nu, NC)), dma((nu,)), dma((2,)),
            dma((nu,)), dma((nu,)), dma((nu,)), dma((nu,)),
            dma((NT,)), dma((NT,)), dma((NT,)), dma((NT,)),
            dma((2,)), dma((2,)), dma((4,)), dma((4,)),
        ],
        compiler_params=pltpu.CompilerParams(
            collective_id=0, has_side_effects=True, vmem_limit_bytes=KERNEL_VMEM
        ),
    )(row_start, col_start, spacing, bands, row_interp, col_interp)
    return pl.pallas_call(
        write_kernel,
        out_shape=(out,) * 3,
        in_specs=[smem] + [in_vmem] * 3,
        out_specs=(anywhere,) * 3,
        scratch_shapes=[
            vmem((TILE, LATE[1] - LATE[0]), F32), vmem((TILE, LATE[1] - LATE[0]), F32),
            dma((5,)), dma((2, 4)),
        ],
        compiler_params=pltpu.CompilerParams(vmem_limit_bytes=8 * 2**20),
    )(spacing, z, vs, vh)


def solution(mesh):
    in_specs = (
        P(("band", "col"), None),
        P("band", None, None),
        P("col", None, None),
        P("band"),
        P("col"),
        P("band"),
    )
    out_specs = (P("band", "col"), P("band", "col"), P("band", "col"))
    return jax.shard_map(
        on_device, mesh=mesh, in_specs=in_specs, out_specs=out_specs, check_vma=False
    )
```

```python
import jax
import jax.numpy as jnp
from jax import lax
from jax.experimental import pallas as pl
from jax.experimental.pallas import tpu as pltpu
from jax.sharding import PartitionSpec as P

MESH = pl.DeviceIdType.MESH
F32, BF16 = jnp.float32, jnp.bfloat16

TILE, WIN, MARGIN = 512, 640, 128
NB, NC, NT = 16, 8, 4
COLS = 16384
BLOCK = TILE * NT
SPAN = TILE + 2 * MARGIN
EXT = BLOCK + 2 * MARGIN
SRC = TILE // NC
Z = TILE + 16

UNITS = (
    (0, 128, 256),
    (256, 512),
    (512, 768),
    (1536, 1792),
    (1792, 2048),
    (2048, 2176, 2304),
    (768, 1024),
    (1024, 1280),
    (1280, 1536),
)
WIDE = 256
AHEAD = 2
DONE = {2: 0, 5: 3, 7: 1, 8: 2}
MAKE = {0: 0, 1: 3, 2: 1, 3: 2}
HORN = {4: (0, ((128, 384),)), 6: (3, ((0, 128), (1664, 2048))), 8: (1, ((384, 896),))}
LATE = (896, 1664)
FROM = NB // 2 - 1
PARTS = 4
SLICE = MARGIN // PARTS
VIA_DOWN = (10, 12, 14)
VIA_UP = (1, 3, 5)
KERNEL_VMEM = 47 * 2**20
TINY = 1.1754944e-38


def split(x):
    high = x.astype(BF16)
    return high, (x - high.astype(F32)).astype(BF16)


def dot(a, b):
    return lax.dot_general(a, b, (((1,), (0,)), ((), ())), preferred_element_type=F32)


def dot3(ah, al, bh, bl):
    return dot(ah, bh) + dot(ah, bl) + dot(al, bh)


def horn(z, inv, r, lo, width):
    span = width + 2 * MARGIN
    blk = z[pl.ds(r, 32), lo : lo + span]
    up, mid, dn = blk[7:23], blk[8:24], blk[9:25]
    s = up + dn + 2.0 * mid
    d = dn - up
    sc = jnp.tile(inv, (1, width // 128))
    keep = slice(MARGIN, MARGIN + width)
    p = (pltpu.roll(s, span - 1, 1) - pltpu.roll(s, 1, 1))[:, keep] * sc
    q = (pltpu.roll(d, span - 1, 1) + pltpu.roll(d, 1, 1) + 2.0 * d)[:, keep] * sc
    t = p * p + q * q
    u = 1.0 + t
    f = lax.rsqrt(u)
    return t * lax.rsqrt(jnp.maximum(t * u, TINY)), (0.70710678 + 0.5 * (q - p)) * f


def inverse(spacing):
    return 1.0 / jnp.full((16, 128), 8.0 * spacing[0], F32)


def gather_kernel(
    row_start, col_start, spacing, bands, row_interp, col_interp,
    z, vs, vh,
    ext, rmat, cmat, rh, rl, ch, cl, wh, wl, left, right, lsend, rsend, hold, acc,
    send_sem, recv_sem, own_sem, mat_sem, up_send, up_recv, dn_send, dn_recv,
    eu_send, eu_recv, ed_send, ed_recv, side_send, side_recv, corner_send, corner_recv, hold_send, hold_recv,
):
    b, c = lax.axis_index("band"), lax.axis_index("col")
    zh, y = c // 4, lax.rem(c, 4)

    def peer(s):
        return lax.rem(zh + lax.rem(s, 2), 2) * 4 + lax.rem(y + s // 2, 4)

    def at(db, dc):
        return {"band": b + db, "col": c + dc}

    def exists(db, dc):
        ok = jnp.bool_(True)
        if db < 0:
            ok = b > 0
        if db > 0:
            ok = b < NB - 1
        if dc < 0:
            ok = jnp.logical_and(ok, c > 0)
        if dc > 0:
            ok = jnp.logical_and(ok, c < NC - 1)
        return ok

    z[0:8, :] = jnp.zeros((8, EXT), F32)
    z[Z - 8 : Z, :] = jnp.zeros((8, EXT), F32)
    left[...] = jnp.zeros_like(left)
    right[...] = jnp.zeros_like(right)

    barrier = pltpu.get_barrier_semaphore()

    def greet(s, carry):
        pl.semaphore_signal(barrier, 1, device_id={"col": peer(s)}, device_id_type=MESH)
        return carry

    lax.fori_loop(1, NC, greet, 0)
    near = [(db, dc) for db in (-1, 1) for dc in (-1, 0, 1)]
    for db, dc in near:
        @pl.when(exists(db, dc))
        def _():
            pl.semaphore_signal(barrier, 1, device_id=at(db, dc), device_id_type=MESH)
    via_down = jnp.logical_and(b >= VIA_DOWN[0], jnp.logical_and(b <= VIA_DOWN[-1], lax.rem(b, 2) == 0))
    via_up = jnp.logical_and(b <= VIA_UP[-1], lax.rem(b, 2) == 1)
    via = jnp.logical_or(via_down, via_up)
    ends = jnp.logical_or(b == FROM, b == FROM + 1)
    for other in (FROM, FROM + 1):
        @pl.when(via)
        def _():
            pl.semaphore_signal(barrier, 1, device_id={"band": other, "col": c}, device_id_type=MESH)
    for other in VIA_DOWN + VIA_UP:
        @pl.when(ends)
        def _():
            pl.semaphore_signal(barrier, 1, device_id={"band": other, "col": c}, device_id_type=MESH)
    extra = 2 * via.astype(jnp.int32) + 6 * ends.astype(jnp.int32)
    rows_near = (b > 0).astype(jnp.int32) + (b < NB - 1).astype(jnp.int32)
    cols_near = (c > 0).astype(jnp.int32) + (c < NC - 1).astype(jnp.int32)
    pl.semaphore_wait(barrier, NC - 1 + rows_near * (1 + cols_near) + extra)

    mine = pl.ds(pl.multiple_of(c * SRC, SRC), SRC)
    def post(g):
        edges = UNITS[g]
        for lo, hi in zip(edges[:-1], edges[1:]):
            def source(dst, lo=lo, hi=hi):
                start = lax.rem(dst * BLOCK + (lo + COLS - MARGIN), COLS)
                return bands.at[:, pl.ds(pl.multiple_of(start, 128), hi - lo)]

            def send(s, carry, lo=lo, hi=hi, source=source):
                dst = peer(s)
                pltpu.make_async_remote_copy(
                    source(dst), ext.at[mine, lo:hi], send_sem.at[g], recv_sem.at[g, c],
                    device_id={"col": dst}, device_id_type=MESH,
                ).start()
                return carry

            lax.fori_loop(1, NC, send, 0)
            pltpu.make_async_copy(source(c), ext.at[mine, lo:hi], own_sem.at[g]).start()

    for g in range(AHEAD):
        post(g)

    rcopy = pltpu.make_async_copy(row_interp.at[0], rmat, mat_sem.at[0])
    ccopy = pltpu.make_async_copy(col_interp, cmat, mat_sem.at[1])
    rcopy.start()
    ccopy.start()

    @pl.when(b == 0)
    def _():
        ext[TILE : TILE + MARGIN, :] = jnp.zeros((MARGIN, EXT), F32)

    @pl.when(b == NB - 1)
    def _():
        ext[TILE + MARGIN :, :] = jnp.zeros((MARGIN, EXT), F32)

    rcopy.wait()
    ah, al = split(rmat[...])
    r0 = row_start[0]
    for k in range(3):
        m = lax.broadcasted_iota(jnp.int32, (WIN, 256), 1) + k * 256
        row = m + MARGIN if k < 2 else jnp.where(m < TILE + MARGIN, m - TILE, m)
        hot = jnp.where(row - r0 == lax.broadcasted_iota(jnp.int32, (WIN, 256), 0), 1.0, 0.0).astype(BF16)
        rh[:, k * 256 : (k + 1) * 256] = dot(ah, hot).astype(BF16)
        rl[:, k * 256 : (k + 1) * 256] = dot(al, hot).astype(BF16)

    def make(j):
        if j == MAKE[0]:
            ccopy.wait()
        c0 = col_start[j]
        low = jnp.where(c == 0, MARGIN, 0) if j == 0 else 0
        high = jnp.where(c == NC - 1, TILE + MARGIN, SPAN) if j == NT - 1 else SPAN

        def move(k, carry):
            base = pl.multiple_of(k * 256, 256)
            ah, al = split(cmat[j])
            m = lax.broadcasted_iota(jnp.int32, (256, WIN), 0) + base
            hit = m - c0 == lax.broadcasted_iota(jnp.int32, (256, WIN), 1)
            hit = jnp.logical_and(hit, jnp.logical_and(m >= low, m < high))
            hot = jnp.where(hit, 1.0, 0.0).astype(BF16)
            ch[j, pl.ds(base, 256), :] = dot(hot, ah).astype(BF16)
            cl[j, pl.ds(base, 256), :] = dot(hot, al).astype(BF16)
            return carry

        lax.fori_loop(0, SPAN // 256, move, 0)

    inv = inverse(spacing)

    def edge(ref_from, ref_to, sends, recvs, db, dc):
        return pltpu.make_async_remote_copy(
            ref_from, ref_to, sends, recvs, device_id=at(db, dc), device_id_type=MESH
        )

    def relays(g):
        cols = slice(UNITS[g][0], UNITS[g][-1])
        down = edge(ext.at[TILE - MARGIN : TILE, cols], ext.at[TILE : TILE + MARGIN, cols], dn_send.at[g], dn_recv.at[g], 1, 0)
        upward = edge(ext.at[0:MARGIN, cols], ext.at[TILE + MARGIN : SPAN, cols], up_send.at[g], up_recv.at[g], -1, 0)
        return down, upward

    def arrive(g):
        cols = slice(UNITS[g][0], UNITS[g][-1])

        def one(s, carry):
            src = peer(s)
            rows = ext.at[pl.ds(pl.multiple_of(src * SRC, SRC), SRC), cols]
            pltpu.make_async_remote_copy(
                rows, rows, send_sem.at[g], recv_sem.at[g, src], device_id={"col": src}, device_id_type=MESH
            ).wait_recv()
            return carry

        lax.fori_loop(1, NC, one, 0)
        pltpu.make_async_copy(ext.at[mine, cols], ext.at[mine, cols], own_sem.at[g]).wait()
        down, upward = relays(g)
        if g == len(UNITS) - 1:
            pl.when(b < NB - 1)(down.start)
            pl.when(b > 0)(upward.start)
        else:
            pl.when(jnp.logical_and(b < NB - 1, b != FROM))(down.start)
            pl.when(jnp.logical_and(b > 0, b != FROM + 1))(upward.start)
            for at_band, base, to, direct, others, sends, recvs in (
                (FROM, TILE - MARGIN, TILE, FROM + 1, VIA_DOWN, dn_send, dn_recv),
                (FROM + 1, 0, TILE + MARGIN, FROM, VIA_UP, up_send, up_recv),
            ):
                @pl.when(b == at_band)
                def _():
                    for i in range(PARTS):
                        part = slice(base + i * SLICE, base + (i + 1) * SLICE)
                        pltpu.make_async_remote_copy(
                            ext.at[part, cols],
                            hold.at[:, cols] if i else ext.at[to : to + SLICE, cols],
                            sends.at[g], hold_recv.at[g] if i else recvs.at[g],
                            device_id={"band": others[i - 1] if i else direct, "col": c}, device_id_type=MESH,
                        ).start()
        if g + AHEAD < len(UNITS):
            post(g + AHEAD)

    def forwards(g):
        cols = slice(UNITS[g][0], UNITS[g][-1])
        made = []
        for to, start, dest, recvs in (
            (FROM + 1, TILE + (b - FROM - 1) // 2 * SLICE, via_down, dn_recv),
            (FROM, TILE + MARGIN + (b + 1) // 2 * SLICE, via_up, up_recv),
        ):
            copy = pltpu.make_async_remote_copy(
                hold.at[:, cols], ext.at[pl.ds(pl.multiple_of(start, SLICE), SLICE), cols], hold_send.at[g], recvs.at[g],
                device_id={"band": to, "col": c}, device_id_type=MESH,
            )
            made.append((dest, copy))
        return made

    def forward(g):
        for chosen, copy in forwards(g):
            @pl.when(chosen)
            def _():
                pltpu.make_async_remote_copy(
                    hold.at[:, UNITS[g][0] : UNITS[g][-1]], hold.at[:, UNITS[g][0] : UNITS[g][-1]],
                    hold_send.at[g], hold_recv.at[g], device_id={"band": FROM, "col": c}, device_id_type=MESH,
                ).wait_recv()
                copy.start()

    def finish(pairs):
        for copy, way in pairs:
            pl.when(exists(-way[0], -way[1]))(copy.wait_recv)
            pl.when(exists(*way))(copy.wait_send)

    waits = {}

    def complete(tile):
        def cols_of(n, carry):
            at_n = pl.ds(pl.multiple_of(n * 256, 256), 256)
            part = dot3(wh[:, tile * TILE : tile * TILE + SPAN], wl[:, tile * TILE : tile * TILE + SPAN], ch[tile, :, at_n], cl[tile, :, at_n])
            z[8 : 8 + TILE, pl.ds(pl.multiple_of(MARGIN + tile * TILE + n * 256, 128), 256)] = part
            return carry

        lax.fori_loop(0, TILE // 256, cols_of, 0)

        tc = slice(MARGIN + tile * TILE, MARGIN + (tile + 1) * TILE)
        first, last = slice(8, 16), slice(TILE, TILE + 8)
        top, bottom = slice(0, 8), slice(Z - 8, Z)
        pairs = [
            (edge(z.at[last, tc], z.at[top, tc], ed_send.at[tile], ed_recv.at[tile], 1, 0), (1, 0)),
            (edge(z.at[first, tc], z.at[bottom, tc], eu_send.at[tile], eu_recv.at[tile], -1, 0), (-1, 0)),
        ]
        if tile == 0:
            near_cols, far_cols, dc = slice(MARGIN, 2 * MARGIN), slice(EXT - MARGIN, EXT), -1
            lsend[...] = jnp.transpose(z[8 : 8 + TILE, near_cols])[0:8, :]
            pairs.append((edge(lsend, right.at[0:8, :], side_send.at[0], side_recv.at[0], 0, -1), (0, -1)))
        if tile == NT - 1:
            near_cols, far_cols, dc = slice(BLOCK, BLOCK + MARGIN), slice(0, MARGIN), 1
            rsend[...] = jnp.transpose(z[8 : 8 + TILE, near_cols])[120:128, :]
            pairs.append((edge(rsend, left.at[120:128, :], side_send.at[1], side_recv.at[1], 0, 1), (0, 1)))
        if tile in (0, NT - 1):
            i = 0 if tile == 0 else 2
            pairs.append((edge(z.at[last, near_cols], z.at[top, far_cols], corner_send.at[i], corner_recv.at[i], 1, dc), (1, dc)))
            pairs.append((edge(z.at[first, near_cols], z.at[bottom, far_cols], corner_send.at[i + 1], corner_recv.at[i + 1], -1, dc), (-1, dc)))
        for copy, way in pairs:
            pl.when(exists(*way))(copy.start)
        waits[tile] = pairs

    def main_rows(g):
        lo, hi = UNITS[g][0], UNITS[g][-1]
        xh, xl = split(ext[0:TILE, lo:hi])
        acc[g % 2] = dot3(rh[:, 0:TILE], rl[:, 0:TILE], xh, xl)

    arrive(0)
    main_rows(0)
    for g in range(len(UNITS)):
        lo, hi = UNITS[g][0], UNITS[g][-1]
        tile = DONE.get(g)
        if g + 1 < len(UNITS):
            forward(g)
            arrive(g + 1)
            main_rows(g + 1)
        down, upward = relays(g)
        pl.when(b > 0)(down.wait_recv)
        pl.when(b < NB - 1)(upward.wait_recv)

        xh, xl = split(ext[TILE:, lo:hi])
        part = acc[g % 2] + dot3(rh[:, TILE:], rl[:, TILE:], xh, xl)
        wh[:, lo:hi], wl[:, lo:hi] = split(part)
        if g in MAKE:
            make(MAKE[g])
        if tile is not None:
            complete(tile)
        if g in HORN:
            ready, spans = HORN[g]
            finish(waits.pop(ready))
            if ready == NT - 1:
                z[8 : 8 + TILE, 0:MARGIN] = jnp.transpose(left[...])
                z[8 : 8 + TILE, EXT - MARGIN : EXT] = jnp.transpose(right[...])

            def strip(i, carry):
                r = pl.multiple_of(i * 16, 16)
                for first_col, last_col in spans:
                    o = (pl.ds(r, 16), slice(first_col, last_col))
                    vs[o], vh[o] = horn(z, inv, r, first_col, last_col - first_col)
                return carry

            lax.fori_loop(0, TILE // 16, strip, 0)

    for pairs in waits.values():
        finish(pairs)
    for g in range(len(UNITS)):
        cols = slice(UNITS[g][0], UNITS[g][-1])
        gone = ext.at[0 : (NC - 1) * SRC, cols]
        pltpu.make_async_remote_copy(
            gone, gone, send_sem.at[g], recv_sem.at[g, c], device_id={"col": peer(1)}, device_id_type=MESH
        ).wait_send()
        down, upward = relays(g)
        pl.when(b < NB - 1)(down.wait_send)
        pl.when(b > 0)(upward.wait_send)
        if g + 1 < len(UNITS):
            for chosen, copy in forwards(g):
                pl.when(chosen)(copy.wait_send)


def write_kernel(spacing, z, vs, vh, oz, osl, ohi, hs, hh, sem, late_sem):
    copies = [pltpu.make_async_copy(z.at[8 : 8 + TILE, MARGIN : MARGIN + BLOCK], oz, sem.at[4])]
    for k, (v, o) in enumerate(((vs, osl), (vh, ohi))):
        for n, cs in enumerate((slice(0, LATE[0]), slice(LATE[1], BLOCK))):
            copies.append(pltpu.make_async_copy(v.at[:, cs], o.at[:, cs], sem.at[2 * k + n]))
    for copy in copies:
        copy.start()
    inv = inverse(spacing)
    parts = 4
    for part in range(parts):
        def strip(i, carry):
            r = pl.multiple_of(i * 16, 16)
            for lo in range(LATE[0], LATE[1], 384):
                o = (pl.ds(r, 16), slice(lo - LATE[0], lo - LATE[0] + 384))
                hs[o], hh[o] = horn(z, inv, r, lo, 384)
            return carry

        first, last = part * TILE // parts, (part + 1) * TILE // parts
        lax.fori_loop(first // 16, last // 16, strip, 0)
        for k, (v, o) in enumerate(((hs, osl), (hh, ohi))):
            copy = pltpu.make_async_copy(v.at[first:last], o.at[first:last, LATE[0] : LATE[1]], late_sem.at[k, part])
            copy.start()
            copies.append(copy)
    for copy in copies:
        copy.wait()


def on_device(bands, row_interp, col_interp, row_start, col_start, spacing):
    out = jax.ShapeDtypeStruct((TILE, BLOCK), F32)
    smem, anywhere = pl.BlockSpec(memory_space=pltpu.SMEM), pl.BlockSpec(memory_space=pl.ANY)
    vmem, dma = pltpu.VMEM, pltpu.SemaphoreType.DMA
    nu = len(UNITS)
    in_vmem = pl.BlockSpec(memory_space=pltpu.VMEM)
    z, vs, vh = pl.pallas_call(
        gather_kernel,
        out_shape=(vmem((Z, EXT), F32), vmem((TILE, BLOCK), F32), vmem((TILE, BLOCK), F32)),
        in_specs=[smem] * 3 + [anywhere] * 3,
        out_specs=(in_vmem,) * 3,
        scratch_shapes=[
            vmem((SPAN, EXT), F32),
            vmem((TILE, WIN), F32), vmem((NT, WIN, TILE), F32),
            vmem((TILE, SPAN), BF16), vmem((TILE, SPAN), BF16),
            vmem((NT, SPAN, TILE), BF16), vmem((NT, SPAN, TILE), BF16),
            vmem((TILE, EXT), BF16), vmem((TILE, EXT), BF16),
            vmem((MARGIN, TILE), F32), vmem((MARGIN, TILE), F32),
            vmem((8, TILE), F32), vmem((8, TILE), F32), vmem((SLICE, EXT), F32), vmem((2, TILE, WIDE), F32),
            dma((nu,)), dma((nu, NC)), dma((nu,)), dma((2,)),
            dma((nu,)), dma((nu,)), dma((nu,)), dma((nu,)),
            dma((NT,)), dma((NT,)), dma((NT,)), dma((NT,)),
            dma((2,)), dma((2,)), dma((4,)), dma((4,)), dma((nu,)), dma((nu,)),
        ],
        compiler_params=pltpu.CompilerParams(
            collective_id=0, has_side_effects=True, vmem_limit_bytes=KERNEL_VMEM
        ),
    )(row_start, col_start, spacing, bands, row_interp, col_interp)
    return pl.pallas_call(
        write_kernel,
        out_shape=(out,) * 3,
        in_specs=[smem] + [in_vmem] * 3,
        out_specs=(anywhere,) * 3,
        scratch_shapes=[
            vmem((TILE, LATE[1] - LATE[0]), F32), vmem((TILE, LATE[1] - LATE[0]), F32),
            dma((5,)), dma((2, 4)),
        ],
        compiler_params=pltpu.CompilerParams(vmem_limit_bytes=8 * 2**20),
    )(spacing, z, vs, vh)


def solution(mesh):
    in_specs = (
        P(("band", "col"), None),
        P("band", None, None),
        P("col", None, None),
        P("band"),
        P("col"),
        P("band"),
    )
    out_specs = (P("band", "col"), P("band", "col"), P("band", "col"))
    return jax.shard_map(
        on_device, mesh=mesh, in_specs=in_specs, out_specs=out_specs, check_vma=False
    )
```

```python
import jax
import jax.numpy as jnp
from jax import lax
from jax.experimental import pallas as pl
from jax.experimental.pallas import tpu as pltpu
from jax.sharding import PartitionSpec as P

MESH = pl.DeviceIdType.MESH
F32, BF16 = jnp.float32, jnp.bfloat16

TILE, WIN, MARGIN = 512, 640, 128
NB, NC, NT = 16, 8, 4
COLS = 16384
BLOCK = TILE * NT
SPAN = TILE + 2 * MARGIN
EXT = BLOCK + 2 * MARGIN
SRC = TILE // NC
Z = TILE + 16

UNITS = (
    (0, 128, 256),
    (256, 512),
    (512, 768),
    (1536, 1792),
    (1792, 2048),
    (2048, 2176, 2304),
    (768, 1024),
    (1024, 1280),
    (1280, 1536),
)
WIDE = 256
STRIP = 32
AHEAD = 2
DONE = {2: 0, 5: 3, 7: 1, 8: 2}
MAKE = {0: 0, 1: 3, 2: 1, 3: 2}
HORN = {4: (0, ((128, 384),)), 6: (3, ((0, 128), (1664, 2048))), 8: (1, ((384, 896),))}
LATE = (896, 1664)
FROM = NB // 2 - 1
PARTS = 4
SLICE = MARGIN // PARTS
VIA_DOWN = (10, 12, 14)
VIA_UP = (1, 3, 5)
KERNEL_VMEM = 47 * 2**20
TINY = 1.1754944e-38


def split(x):
    high = x.astype(BF16)
    return high, (x - high.astype(F32)).astype(BF16)


def dot(a, b):
    return lax.dot_general(a, b, (((1,), (0,)), ((), ())), preferred_element_type=F32)


def dot3(ah, al, bh, bl):
    return dot(ah, bh) + dot(ah, bl) + dot(al, bh)


def horn(z, inv, r, lo, width):
    span = width + 2 * MARGIN
    blk = z[pl.ds(r, STRIP + 16), lo : lo + span]
    up, mid, dn = (blk[k : k + STRIP] for k in (7, 8, 9))
    s = up + dn + 2.0 * mid
    d = dn - up
    sc = jnp.tile(inv, (1, width // 128))
    keep = slice(MARGIN, MARGIN + width)
    p = (pltpu.roll(s, span - 1, 1) - pltpu.roll(s, 1, 1))[:, keep] * sc
    q = (pltpu.roll(d, span - 1, 1) + pltpu.roll(d, 1, 1) + 2.0 * d)[:, keep] * sc
    t = p * p + q * q
    u = 1.0 + t
    f = lax.rsqrt(u)
    return t * lax.rsqrt(jnp.maximum(t * u, TINY)), (0.70710678 + 0.5 * (q - p)) * f


def inverse(spacing):
    return 1.0 / jnp.full((STRIP, 128), 8.0 * spacing[0], F32)


def gather_kernel(
    row_start, col_start, spacing, bands, row_interp, col_interp,
    z, vs, vh,
    ext, rmat, cmat, rh, rl, ch, cl, wh, wl, left, right, lsend, rsend, hold, acc,
    send_sem, recv_sem, own_sem, mat_sem, up_send, up_recv, dn_send, dn_recv,
    eu_send, eu_recv, ed_send, ed_recv, side_send, side_recv, corner_send, corner_recv, hold_send, hold_recv,
):
    b, c = lax.axis_index("band"), lax.axis_index("col")
    zh, y = c // 4, lax.rem(c, 4)

    def peer(s):
        return lax.rem(zh + lax.rem(s, 2), 2) * 4 + lax.rem(y + s // 2, 4)

    def at(db, dc):
        return {"band": b + db, "col": c + dc}

    def exists(db, dc):
        ok = jnp.bool_(True)
        if db < 0:
            ok = b > 0
        if db > 0:
            ok = b < NB - 1
        if dc < 0:
            ok = jnp.logical_and(ok, c > 0)
        if dc > 0:
            ok = jnp.logical_and(ok, c < NC - 1)
        return ok

    z[0:8, :] = jnp.zeros((8, EXT), F32)
    z[Z - 8 : Z, :] = jnp.zeros((8, EXT), F32)
    left[...] = jnp.zeros_like(left)
    right[...] = jnp.zeros_like(right)

    barrier = pltpu.get_barrier_semaphore()

    def greet(s, carry):
        pl.semaphore_signal(barrier, 1, device_id={"col": peer(s)}, device_id_type=MESH)
        return carry

    lax.fori_loop(1, NC, greet, 0)
    near = [(db, dc) for db in (-1, 1) for dc in (-1, 0, 1)]
    for db, dc in near:
        @pl.when(exists(db, dc))
        def _():
            pl.semaphore_signal(barrier, 1, device_id=at(db, dc), device_id_type=MESH)
    via_down = jnp.logical_and(b >= VIA_DOWN[0], jnp.logical_and(b <= VIA_DOWN[-1], lax.rem(b, 2) == 0))
    via_up = jnp.logical_and(b <= VIA_UP[-1], lax.rem(b, 2) == 1)
    via = jnp.logical_or(via_down, via_up)
    ends = jnp.logical_or(b == FROM, b == FROM + 1)
    for other in (FROM, FROM + 1):
        @pl.when(via)
        def _():
            pl.semaphore_signal(barrier, 1, device_id={"band": other, "col": c}, device_id_type=MESH)
    for other in VIA_DOWN + VIA_UP:
        @pl.when(ends)
        def _():
            pl.semaphore_signal(barrier, 1, device_id={"band": other, "col": c}, device_id_type=MESH)
    extra = 2 * via.astype(jnp.int32) + 6 * ends.astype(jnp.int32)
    rows_near = (b > 0).astype(jnp.int32) + (b < NB - 1).astype(jnp.int32)
    cols_near = (c > 0).astype(jnp.int32) + (c < NC - 1).astype(jnp.int32)
    pl.semaphore_wait(barrier, NC - 1 + rows_near * (1 + cols_near) + extra)

    mine = pl.ds(pl.multiple_of(c * SRC, SRC), SRC)
    def post(g):
        edges = UNITS[g]
        for lo, hi in zip(edges[:-1], edges[1:]):
            def source(dst, lo=lo, hi=hi):
                start = lax.rem(dst * BLOCK + (lo + COLS - MARGIN), COLS)
                return bands.at[:, pl.ds(pl.multiple_of(start, 128), hi - lo)]

            def send(s, carry, lo=lo, hi=hi, source=source):
                dst = peer(s)
                pltpu.make_async_remote_copy(
                    source(dst), ext.at[mine, lo:hi], send_sem.at[g], recv_sem.at[g, c],
                    device_id={"col": dst}, device_id_type=MESH,
                ).start()
                return carry

            lax.fori_loop(1, NC, send, 0)
            pltpu.make_async_copy(source(c), ext.at[mine, lo:hi], own_sem.at[g]).start()

    for g in range(AHEAD):
        post(g)

    rcopy = pltpu.make_async_copy(row_interp.at[0], rmat, mat_sem.at[0])
    ccopy = pltpu.make_async_copy(col_interp, cmat, mat_sem.at[1])
    rcopy.start()
    ccopy.start()

    @pl.when(b == 0)
    def _():
        ext[TILE : TILE + MARGIN, :] = jnp.zeros((MARGIN, EXT), F32)

    @pl.when(b == NB - 1)
    def _():
        ext[TILE + MARGIN :, :] = jnp.zeros((MARGIN, EXT), F32)

    rcopy.wait()
    ah, al = split(rmat[...])
    r0 = row_start[0]
    for k in range(3):
        m = lax.broadcasted_iota(jnp.int32, (WIN, 256), 1) + k * 256
        row = m + MARGIN if k < 2 else jnp.where(m < TILE + MARGIN, m - TILE, m)
        hot = jnp.where(row - r0 == lax.broadcasted_iota(jnp.int32, (WIN, 256), 0), 1.0, 0.0).astype(BF16)
        rh[:, k * 256 : (k + 1) * 256] = dot(ah, hot).astype(BF16)
        rl[:, k * 256 : (k + 1) * 256] = dot(al, hot).astype(BF16)

    def make(j):
        if j == MAKE[0]:
            ccopy.wait()
        c0 = col_start[j]
        low = jnp.where(c == 0, MARGIN, 0) if j == 0 else 0
        high = jnp.where(c == NC - 1, TILE + MARGIN, SPAN) if j == NT - 1 else SPAN

        def move(k, carry):
            base = pl.multiple_of(k * 256, 256)
            ah, al = split(cmat[j])
            m = lax.broadcasted_iota(jnp.int32, (256, WIN), 0) + base
            hit = m - c0 == lax.broadcasted_iota(jnp.int32, (256, WIN), 1)
            hit = jnp.logical_and(hit, jnp.logical_and(m >= low, m < high))
            hot = jnp.where(hit, 1.0, 0.0).astype(BF16)
            ch[j, pl.ds(base, 256), :] = dot(hot, ah).astype(BF16)
            cl[j, pl.ds(base, 256), :] = dot(hot, al).astype(BF16)
            return carry

        lax.fori_loop(0, SPAN // 256, move, 0)

    inv = inverse(spacing)

    def edge(ref_from, ref_to, sends, recvs, db, dc):
        return pltpu.make_async_remote_copy(
            ref_from, ref_to, sends, recvs, device_id=at(db, dc), device_id_type=MESH
        )

    def relays(g):
        cols = slice(UNITS[g][0], UNITS[g][-1])
        down = edge(ext.at[TILE - MARGIN : TILE, cols], ext.at[TILE : TILE + MARGIN, cols], dn_send.at[g], dn_recv.at[g], 1, 0)
        upward = edge(ext.at[0:MARGIN, cols], ext.at[TILE + MARGIN : SPAN, cols], up_send.at[g], up_recv.at[g], -1, 0)
        return down, upward

    def arrive(g):
        cols = slice(UNITS[g][0], UNITS[g][-1])

        def one(s, carry):
            src = peer(s)
            rows = ext.at[pl.ds(pl.multiple_of(src * SRC, SRC), SRC), cols]
            pltpu.make_async_remote_copy(
                rows, rows, send_sem.at[g], recv_sem.at[g, src], device_id={"col": src}, device_id_type=MESH
            ).wait_recv()
            return carry

        lax.fori_loop(1, NC, one, 0)
        pltpu.make_async_copy(ext.at[mine, cols], ext.at[mine, cols], own_sem.at[g]).wait()
        down, upward = relays(g)
        if g == len(UNITS) - 1:
            pl.when(b < NB - 1)(down.start)
            pl.when(b > 0)(upward.start)
        else:
            pl.when(jnp.logical_and(b < NB - 1, b != FROM))(down.start)
            pl.when(jnp.logical_and(b > 0, b != FROM + 1))(upward.start)
            for at_band, base, to, direct, others, sends, recvs in (
                (FROM, TILE - MARGIN, TILE, FROM + 1, VIA_DOWN, dn_send, dn_recv),
                (FROM + 1, 0, TILE + MARGIN, FROM, VIA_UP, up_send, up_recv),
            ):
                @pl.when(b == at_band)
                def _():
                    for i in range(PARTS):
                        part = slice(base + i * SLICE, base + (i + 1) * SLICE)
                        pltpu.make_async_remote_copy(
                            ext.at[part, cols],
                            hold.at[:, cols] if i else ext.at[to : to + SLICE, cols],
                            sends.at[g], hold_recv.at[g] if i else recvs.at[g],
                            device_id={"band": others[i - 1] if i else direct, "col": c}, device_id_type=MESH,
                        ).start()
        if g + AHEAD < len(UNITS):
            post(g + AHEAD)

    def forwards(g):
        cols = slice(UNITS[g][0], UNITS[g][-1])
        made = []
        for to, start, dest, recvs in (
            (FROM + 1, TILE + (b - FROM - 1) // 2 * SLICE, via_down, dn_recv),
            (FROM, TILE + MARGIN + (b + 1) // 2 * SLICE, via_up, up_recv),
        ):
            copy = pltpu.make_async_remote_copy(
                hold.at[:, cols], ext.at[pl.ds(pl.multiple_of(start, SLICE), SLICE), cols], hold_send.at[g], recvs.at[g],
                device_id={"band": to, "col": c}, device_id_type=MESH,
            )
            made.append((dest, copy))
        return made

    def forward(g):
        for chosen, copy in forwards(g):
            @pl.when(chosen)
            def _():
                pltpu.make_async_remote_copy(
                    hold.at[:, UNITS[g][0] : UNITS[g][-1]], hold.at[:, UNITS[g][0] : UNITS[g][-1]],
                    hold_send.at[g], hold_recv.at[g], device_id={"band": FROM, "col": c}, device_id_type=MESH,
                ).wait_recv()
                copy.start()

    def finish(pairs):
        for copy, way in pairs:
            pl.when(exists(-way[0], -way[1]))(copy.wait_recv)
            pl.when(exists(*way))(copy.wait_send)

    waits = {}

    def complete(tile):
        def cols_of(n, carry):
            at_n = pl.ds(pl.multiple_of(n * 256, 256), 256)
            part = dot3(wh[:, tile * TILE : tile * TILE + SPAN], wl[:, tile * TILE : tile * TILE + SPAN], ch[tile, :, at_n], cl[tile, :, at_n])
            z[8 : 8 + TILE, pl.ds(pl.multiple_of(MARGIN + tile * TILE + n * 256, 128), 256)] = part
            return carry

        lax.fori_loop(0, TILE // 256, cols_of, 0)

        tc = slice(MARGIN + tile * TILE, MARGIN + (tile + 1) * TILE)
        first, last = slice(8, 16), slice(TILE, TILE + 8)
        top, bottom = slice(0, 8), slice(Z - 8, Z)
        pairs = [
            (edge(z.at[last, tc], z.at[top, tc], ed_send.at[tile], ed_recv.at[tile], 1, 0), (1, 0)),
            (edge(z.at[first, tc], z.at[bottom, tc], eu_send.at[tile], eu_recv.at[tile], -1, 0), (-1, 0)),
        ]
        if tile == 0:
            near_cols, far_cols, dc = slice(MARGIN, 2 * MARGIN), slice(EXT - MARGIN, EXT), -1
            lsend[...] = jnp.transpose(z[8 : 8 + TILE, near_cols])[0:8, :]
            pairs.append((edge(lsend, right.at[0:8, :], side_send.at[0], side_recv.at[0], 0, -1), (0, -1)))
        if tile == NT - 1:
            near_cols, far_cols, dc = slice(BLOCK, BLOCK + MARGIN), slice(0, MARGIN), 1
            rsend[...] = jnp.transpose(z[8 : 8 + TILE, near_cols])[120:128, :]
            pairs.append((edge(rsend, left.at[120:128, :], side_send.at[1], side_recv.at[1], 0, 1), (0, 1)))
        if tile in (0, NT - 1):
            i = 0 if tile == 0 else 2
            pairs.append((edge(z.at[last, near_cols], z.at[top, far_cols], corner_send.at[i], corner_recv.at[i], 1, dc), (1, dc)))
            pairs.append((edge(z.at[first, near_cols], z.at[bottom, far_cols], corner_send.at[i + 1], corner_recv.at[i + 1], -1, dc), (-1, dc)))
        for copy, way in pairs:
            pl.when(exists(*way))(copy.start)
        waits[tile] = pairs

    def main_rows(g):
        lo, hi = UNITS[g][0], UNITS[g][-1]
        xh, xl = split(ext[0:TILE, lo:hi])
        acc[g % 2] = dot3(rh[:, 0:TILE], rl[:, 0:TILE], xh, xl)

    arrive(0)
    main_rows(0)
    for g in range(len(UNITS)):
        lo, hi = UNITS[g][0], UNITS[g][-1]
        tile = DONE.get(g)
        if g + 1 < len(UNITS):
            forward(g)
            arrive(g + 1)
            main_rows(g + 1)
        down, upward = relays(g)
        pl.when(b > 0)(down.wait_recv)
        pl.when(b < NB - 1)(upward.wait_recv)

        xh, xl = split(ext[TILE:, lo:hi])
        part = acc[g % 2] + dot3(rh[:, TILE:], rl[:, TILE:], xh, xl)
        wh[:, lo:hi], wl[:, lo:hi] = split(part)
        if g in MAKE:
            make(MAKE[g])
        if tile is not None:
            complete(tile)
        if g in HORN:
            ready, spans = HORN[g]
            finish(waits.pop(ready))
            if ready == NT - 1:
                z[8 : 8 + TILE, 0:MARGIN] = jnp.transpose(left[...])
                z[8 : 8 + TILE, EXT - MARGIN : EXT] = jnp.transpose(right[...])

            def strip(i, carry):
                r = pl.multiple_of(i * STRIP, STRIP)
                for first_col, last_col in spans:
                    o = (pl.ds(r, STRIP), slice(first_col, last_col))
                    vs[o], vh[o] = horn(z, inv, r, first_col, last_col - first_col)
                return carry

            lax.fori_loop(0, TILE // STRIP, strip, 0)

    for pairs in waits.values():
        finish(pairs)
    for g in range(len(UNITS)):
        cols = slice(UNITS[g][0], UNITS[g][-1])
        gone = ext.at[0 : (NC - 1) * SRC, cols]
        pltpu.make_async_remote_copy(
            gone, gone, send_sem.at[g], recv_sem.at[g, c], device_id={"col": peer(1)}, device_id_type=MESH
        ).wait_send()
        down, upward = relays(g)
        pl.when(b < NB - 1)(down.wait_send)
        pl.when(b > 0)(upward.wait_send)
        if g + 1 < len(UNITS):
            for chosen, copy in forwards(g):
                pl.when(chosen)(copy.wait_send)


def write_kernel(spacing, z, vs, vh, oz, osl, ohi, hs, hh, sem, late_sem):
    copies = [pltpu.make_async_copy(z.at[8 : 8 + TILE, MARGIN : MARGIN + BLOCK], oz, sem.at[4])]
    for k, (v, o) in enumerate(((vs, osl), (vh, ohi))):
        for n, cs in enumerate((slice(0, LATE[0]), slice(LATE[1], BLOCK))):
            copies.append(pltpu.make_async_copy(v.at[:, cs], o.at[:, cs], sem.at[2 * k + n]))
    for copy in copies:
        copy.start()
    inv = inverse(spacing)
    parts = 4
    for part in range(parts):
        def strip(i, carry):
            r = pl.multiple_of(i * STRIP, STRIP)
            for lo in range(LATE[0], LATE[1], 384):
                o = (pl.ds(r, STRIP), slice(lo - LATE[0], lo - LATE[0] + 384))
                hs[o], hh[o] = horn(z, inv, r, lo, 384)
            return carry

        first, last = part * TILE // parts, (part + 1) * TILE // parts
        lax.fori_loop(first // STRIP, last // STRIP, strip, 0)
        for k, (v, o) in enumerate(((hs, osl), (hh, ohi))):
            copy = pltpu.make_async_copy(v.at[first:last], o.at[first:last, LATE[0] : LATE[1]], late_sem.at[k, part])
            copy.start()
            copies.append(copy)
    for copy in copies:
        copy.wait()


def on_device(bands, row_interp, col_interp, row_start, col_start, spacing):
    out = jax.ShapeDtypeStruct((TILE, BLOCK), F32)
    smem, anywhere = pl.BlockSpec(memory_space=pltpu.SMEM), pl.BlockSpec(memory_space=pl.ANY)
    vmem, dma = pltpu.VMEM, pltpu.SemaphoreType.DMA
    nu = len(UNITS)
    in_vmem = pl.BlockSpec(memory_space=pltpu.VMEM)
    z, vs, vh = pl.pallas_call(
        gather_kernel,
        out_shape=(vmem((Z, EXT), F32), vmem((TILE, BLOCK), F32), vmem((TILE, BLOCK), F32)),
        in_specs=[smem] * 3 + [anywhere] * 3,
        out_specs=(in_vmem,) * 3,
        scratch_shapes=[
            vmem((SPAN, EXT), F32),
            vmem((TILE, WIN), F32), vmem((NT, WIN, TILE), F32),
            vmem((TILE, SPAN), BF16), vmem((TILE, SPAN), BF16),
            vmem((NT, SPAN, TILE), BF16), vmem((NT, SPAN, TILE), BF16),
            vmem((TILE, EXT), BF16), vmem((TILE, EXT), BF16),
            vmem((MARGIN, TILE), F32), vmem((MARGIN, TILE), F32),
            vmem((8, TILE), F32), vmem((8, TILE), F32), vmem((SLICE, EXT), F32), vmem((2, TILE, WIDE), F32),
            dma((nu,)), dma((nu, NC)), dma((nu,)), dma((2,)),
            dma((nu,)), dma((nu,)), dma((nu,)), dma((nu,)),
            dma((NT,)), dma((NT,)), dma((NT,)), dma((NT,)),
            dma((2,)), dma((2,)), dma((4,)), dma((4,)), dma((nu,)), dma((nu,)),
        ],
        compiler_params=pltpu.CompilerParams(
            collective_id=0, has_side_effects=True, vmem_limit_bytes=KERNEL_VMEM
        ),
    )(row_start, col_start, spacing, bands, row_interp, col_interp)
    return pl.pallas_call(
        write_kernel,
        out_shape=(out,) * 3,
        in_specs=[smem] + [in_vmem] * 3,
        out_specs=(anywhere,) * 3,
        scratch_shapes=[
            vmem((TILE, LATE[1] - LATE[0]), F32), vmem((TILE, LATE[1] - LATE[0]), F32),
            dma((5,)), dma((2, 4)),
        ],
        compiler_params=pltpu.CompilerParams(vmem_limit_bytes=8 * 2**20),
    )(spacing, z, vs, vh)


def solution(mesh):
    in_specs = (
        P(("band", "col"), None),
        P("band", None, None),
        P("col", None, None),
        P("band"),
        P("col"),
        P("band"),
    )
    out_specs = (P("band", "col"), P("band", "col"), P("band", "col"))
    return jax.shard_map(
        on_device, mesh=mesh, in_specs=in_specs, out_specs=out_specs, check_vma=False
    )
```
